256 devices in a mesh: state: 32 (over x, y, z_lo), group: 8 (over z_hi, core).
Axes of the slice: x: 4, y: 4, z: 8 (z_hi: 4, z_lo: 2; z = z_hi * 2 + z_lo), core: 2. Of those that a mesh axis runs over, the one named last changes fastest.
Arguments:
- basis_rows: bfloat16 [98304, 512], P('state'), may hold values from -6 to 6
- tile_blocks: bfloat16 [32, 8, 32, 6, 128, 128], P('state', 'group'), may hold values from -0.09375 to 0.09375
- tile_cols: int32 [32, 8, 32], P('state', 'group'), may hold values from 0 to 23
- tile_rows: int32 [32, 8, 32, 6], P('state', 'group'), may hold values from 0 to 23, as said below
- tile_counts: int32 [32, 8, 32], P('state', 'group'), may hold values from 1 to 6, as said below
Outputs:
- coupling: float32 [512, 512], P(('state', 'group'))
The draws below stay inside these ranges and needn't reach their ends.
Inputs may be any that keep to these rules, and one draw needn't show every extreme that they name: `tile_rows`: the 6 block-rows of one (s, g, p) are distinct. `tile_counts`: on every device some source shard has all 6 slots live.
All inputs are finite; a program needn't handle non-finite values.
Results may differ from the reference program's by a relative error of at most 0.0003.
Values may be sent and summed in bfloat16 or wider, within the bound.
No kernel may reach another device: no remote copies, remote signals or barrier semaphores. Data moves between devices by JAX's collectives and lax.ppermute only.
A program may use at most 128 MiB of HBM per device.

```python
import math
import jax
import jax.numpy as jnp
from jax import lax

K = 512
B = 128
BLK_DEV = 24
USES = 6
SHARDS = 32
GROUPS = 8
STATES = 98304


def draw_tile_rows(key, part):
    scores = jax.random.randint(key, (SHARDS, GROUPS, SHARDS, BLK_DEV), 0, 1 << 20) * BLK_DEV
    scores = scores + jnp.arange(BLK_DEV, dtype=jnp.int32)
    ranked = jnp.argsort(scores, axis=-1, stable=True)
    return ranked[..., :USES].astype(jnp.int32)


def draw_tile_counts(key, part):
    key_one = jax.random.fold_in(key, 11)
    key_two = jax.random.fold_in(key, 23)
    counts = jax.random.randint(key_one, (SHARDS, GROUPS, SHARDS), 1, USES + 1)
    picked_peer = jax.random.randint(key_two, (SHARDS, GROUPS, 1), 0, SHARDS)
    full_slot = jnp.arange(SHARDS, dtype=jnp.int32)[None, None, :] == picked_peer
    return jnp.where(full_slot, USES, counts).astype(jnp.int32)


def touch_ends(array, stream_key, least, high):
    shape = array.shape
    place = [jax.random.randint(jax.random.fold_in(stream_key, axis), (), 0, shape[axis]) for axis in range(len(shape))]
    array = array.at[tuple(place)].set(least)
    longest = shape.index(max(shape))
    place[longest] = (place[longest] + 1) % shape[longest]
    return array.at[tuple(place)].set(high)


def block_scale(stream_key, extent, pieces, low, top_value):
    factor_of = 1.0
    for dim, shards_of in pieces:
        draws = jax.random.uniform(jax.random.fold_in(jax.random.fold_in(stream_key, 6), dim), (shards_of,), jnp.float32, low / len(pieces), top_value / len(pieces))
        factor_of = factor_of * jnp.repeat(jnp.exp(draws), extent[dim] // shards_of).reshape((-1,) + (1,) * (len(extent) - 1 - dim))
    return factor_of


def normal_values(key, extent, scale, limit, split=(), held_as=jnp.bfloat16):
    level = block_scale(key, extent, split, -0.22, 0.18) if split else 1.0
    drawn = jax.random.normal(key, extent, jnp.float32) * scale * level
    return jnp.minimum(jnp.maximum(drawn, -limit), limit).astype(held_as)


def setup_inputs(seed: int = 0) -> dict:
    seeds = jax.random.split(jax.random.key(seed), 6)
    return {
        "basis_rows": normal_values(seeds[0], (STATES, K), 1.0, 6.0, ((0, 32),)),
        "tile_blocks": normal_values(seeds[1], (SHARDS, GROUPS, SHARDS, USES, B, B), (GROUPS * SHARDS * (USES + 1) * B // (2 * BLK_DEV)) ** -0.5, 0.09375, ((0, 32), (1, 8))),
        "tile_cols": touch_ends(jax.random.randint(seeds[2], (SHARDS, GROUPS, SHARDS), 0, BLK_DEV), jax.random.fold_in(seeds[2], 1), 0, BLK_DEV - 1).astype(jnp.int32),
        "tile_rows": draw_tile_rows(jax.random.fold_in(seeds[5], 71), 0),
        "tile_counts": draw_tile_counts(jax.random.fold_in(seeds[5], 71), 0),
    }


discount = 0.95

def reference(basis_rows, tile_blocks, tile_cols, tile_rows, tile_counts):
    shards = tile_blocks.shape[0]
    groups = tile_blocks.shape[1]
    blocks = basis_rows.reshape(shards * BLK_DEV, B, K)
    peer_index = jnp.arange(shards, dtype=jnp.int32)
    slot_index = jnp.arange(USES, dtype=jnp.int32)

    def visit_device(running, device_id):
        s = device_id // groups
        g = device_id % groups
        tile_set = tile_blocks[s, g].astype(jnp.float32)
        source_cols = (peer_index * BLK_DEV + tile_cols[s, g]).astype(jnp.int32)
        target_rows = (s * BLK_DEV + tile_rows[s, g]).astype(jnp.int32)
        live_mask = (slot_index[None, :] < tile_counts[s, g][:, None]).astype(jnp.float32)
        source_blocks = blocks[source_cols].astype(jnp.float32)
        product = jnp.einsum('puij,pjk->puik', tile_set, source_blocks, precision=lax.Precision.HIGHEST)
        product = product * live_mask[:, :, None, None]
        return (running.at[target_rows].add(product), None)
    running, _ = lax.scan(visit_device, jnp.zeros((shards * BLK_DEV, B, K), jnp.float32), jnp.arange(shards * groups, dtype=jnp.int32))
    stacked = running.reshape(shards * BLK_DEV * B, K)
    basis_wide = basis_rows.astype(jnp.float32)
    gram_part = jnp.dot(basis_rows.T, basis_rows, preferred_element_type=jnp.float32)
    bellman = jnp.dot(basis_wide.T, stacked, precision=lax.Precision.HIGHEST)
    return (gram_part - discount * bellman) * (1.0 / math.sqrt(STATES))
```

```python
import functools
import math

import jax
import jax.numpy as jnp
from jax import lax
from jax.experimental import pallas as pl
from jax.experimental.pallas import tpu as pltpu
from jax.sharding import PartitionSpec as P

discount = 0.95


def tile_kernel(
    start_ref, rows_ref, counts_ref, tiles_ref, phi_ref, high_ref, low_ref, gram_ref, turned
):
    step = pl.program_id(0)
    block_count = phi_ref.shape[0]
    use_count = tiles_ref.shape[1]

    @pl.when(step == 0)
    def _():
        def turn(b, carry):
            turned[b] = phi_ref[b].T
            return carry

        lax.fori_loop(0, block_count, turn, 0)
        gram_ref[...] = jnp.zeros_like(gram_ref)

        def gram(b, carry):
            gram_ref[...] += jnp.dot(turned[b], phi_ref[b], preferred_element_type=jnp.float32)
            return carry

        lax.fori_loop(start_ref[0], start_ref[1], gram, 0)

    count = counts_ref[step]
    left = jnp.concatenate(
        [turned[rows_ref[step * use_count + u]] for u in range(use_count)], axis=1
    )
    right = jnp.concatenate(
        [
            jnp.where(u < count, tiles_ref[0, u], jnp.zeros((), tiles_ref.dtype))
            for u in range(use_count)
        ],
        axis=0,
    )
    product = jnp.dot(left, right, preferred_element_type=jnp.float32) * (-discount)
    high = product.astype(jnp.bfloat16)
    high_ref[...] = high
    low_ref[...] = (product - high.astype(jnp.float32)).astype(jnp.bfloat16)


def apply_tiles(span, rows, counts, tiles, blocks):
    peers, use_count, tile_size, _ = tiles.shape
    block_count, _, features = blocks.shape
    wide = jax.ShapeDtypeStruct((features, peers * tile_size), jnp.bfloat16)
    return pl.pallas_call(
        tile_kernel,
        out_shape=(wide, wide, jax.ShapeDtypeStruct((features, features), jnp.float32)),
        grid_spec=pltpu.PrefetchScalarGridSpec(
            num_scalar_prefetch=3,
            grid=(peers,),
            in_specs=[
                pl.BlockSpec((1, use_count, tile_size, tile_size), lambda p, *_: (p, 0, 0, 0)),
                pl.BlockSpec((block_count, tile_size, features), lambda p, *_: (0, 0, 0)),
            ],
            out_specs=[
                pl.BlockSpec((features, tile_size), lambda p, *_: (0, p)),
                pl.BlockSpec((features, tile_size), lambda p, *_: (0, p)),
                pl.BlockSpec((features, features), lambda p, *_: (0, 0)),
            ],
            scratch_shapes=[pltpu.VMEM((block_count, features, tile_size), jnp.bfloat16)],
        ),
        compiler_params=pltpu.CompilerParams(vmem_limit_bytes=24 << 20),
        cost_estimate=pl.CostEstimate(
            flops=2 * peers * use_count * tile_size * tile_size * features,
            bytes_accessed=2 * tiles.size + 2 * blocks.size + 4 * wide.size,
            transcendentals=0,
        ),
        name="apply_tiles",
    )(span, rows, counts, tiles, blocks)


def join_kernel(high_ref, low_ref, source_ref, gram_ref, out_ref):
    @pl.when(pl.program_id(0) == 0)
    def _():
        out_ref[...] = gram_ref[...]

    source = source_ref[...]
    out_ref[...] += jnp.dot(high_ref[...], source, preferred_element_type=jnp.float32) + jnp.dot(
        low_ref[...], source, preferred_element_type=jnp.float32
    )


def join(high, low, source, gram, steps=8):
    features, depth = high.shape
    chunk = depth // steps
    return pl.pallas_call(
        join_kernel,
        out_shape=jax.ShapeDtypeStruct((features, features), jnp.float32),
        grid=(steps,),
        in_specs=[
            pl.BlockSpec((features, chunk), lambda k: (0, k)),
            pl.BlockSpec((features, chunk), lambda k: (0, k)),
            pl.BlockSpec((chunk, features), lambda k: (k, 0)),
            pl.BlockSpec((features, features), lambda k: (0, 0)),
        ],
        out_specs=pl.BlockSpec((features, features), lambda k: (0, 0)),
        compiler_params=pltpu.CompilerParams(vmem_limit_bytes=16 << 20),
        cost_estimate=pl.CostEstimate(
            flops=4 * features * depth * features,
            bytes_accessed=6 * features * depth,
            transcendentals=0,
        ),
        name="join",
    )(high, low, source, gram)


def body(basis_rows, tile_blocks, tile_cols, tile_rows, tile_counts):
    shards = lax.axis_size("state")
    groups = lax.axis_size("group")
    local_rows, features = basis_rows.shape
    tile_size = tile_blocks.shape[-1]
    block_count = local_rows // tile_size
    blocks = basis_rows.reshape(block_count, tile_size, features)
    exchange = functools.partial(lax.all_to_all, split_axis=0, concat_axis=0, tiled=True)

    asked_cols = exchange(tile_cols[0, 0], "state")
    received = exchange(blocks[asked_cols], "state")

    member = lax.axis_index("group")
    span = jnp.stack([member * block_count // groups, (member + 1) * block_count // groups])
    high, low, gram = apply_tiles(
        span.astype(jnp.int32),
        tile_rows[0, 0].reshape(-1),
        tile_counts[0, 0],
        tile_blocks[0, 0],
        blocks,
    )
    partial = join(high, low, received.reshape(-1, features), gram)

    first = exchange(partial.reshape(shards, features // shards, features), "state").sum(0)
    final = exchange(first.reshape(groups, -1, features), "group").sum(0)
    return final * (1.0 / math.sqrt(local_rows * shards))


def solution(mesh):
    in_specs = (
        P("state", None),
        P("state", "group", None, None, None, None),
        P("state", "group", None),
        P("state", "group", None, None),
        P("state", "group", None),
    )
    out_specs = P(("state", "group"), None)
    return jax.shard_map(body, mesh=mesh, in_specs=in_specs, out_specs=out_specs, check_vma=False)
```

```python
import functools
import math

import jax
import jax.numpy as jnp
from jax import lax
from jax.experimental import pallas as pl
from jax.experimental.pallas import tpu as pltpu
from jax.sharding import PartitionSpec as P


discount = 0.95
extra_rows = 16
first_features = 128
peers_per_step = 4


def dot(left, right):
    return jnp.dot(left, right, preferred_element_type=jnp.float32)


def apply_kernel(
    start, with_cols, rows_ref, counts_ref, cols_ref, tiles_ref, phi_ref, out_ref, turned
):
    step = pl.program_id(0)
    block_count, features, _ = turned.shape
    peers, use_count = tiles_ref.shape[:2]

    @pl.when(step == 0)
    def _():
        def turn(b, carry):
            turned[b] = phi_ref[b, :, start : start + features].T
            return carry

        lax.fori_loop(0, block_count, turn, 0)

    for local in range(peers):
        peer = step * peers + local
        count = counts_ref[peer]
        left = jnp.concatenate(
            [turned[rows_ref[peer * use_count + u]] for u in range(use_count)], axis=1
        )
        right = jnp.concatenate(
            [
                jnp.where(u < count, tiles_ref[local, u], jnp.zeros((), tiles_ref.dtype))
                for u in range(use_count)
            ],
            axis=0,
        )
        product = dot(left, right) * (-discount)
        out_ref[local, :features] = product.astype(out_ref.dtype)
        if with_cols:
            column = jnp.full((extra_rows, out_ref.shape[2]), cols_ref[peer], jnp.int32)
            out_ref[local, features:] = column.astype(jnp.float32).astype(out_ref.dtype)


def apply_tiles(rows, counts, cols, tiles, blocks, start, size, with_cols):
    peers, use_count, tile_size, _ = tiles.shape
    block_count = blocks.shape[0]
    height = size + (extra_rows if with_cols else 0)
    per_step = peers_per_step
    return pl.pallas_call(
        functools.partial(apply_kernel, start, with_cols),
        out_shape=jax.ShapeDtypeStruct((peers, height, tile_size), jnp.bfloat16),
        grid_spec=pltpu.PrefetchScalarGridSpec(
            num_scalar_prefetch=3,
            grid=(peers // per_step,),
            in_specs=[
                pl.BlockSpec(
                    (per_step, use_count, tile_size, tile_size), lambda p, *_: (p, 0, 0, 0)
                ),
                pl.BlockSpec((block_count, tile_size, blocks.shape[2]), lambda p, *_: (0, 0, 0)),
            ],
            out_specs=pl.BlockSpec((per_step, height, tile_size), lambda p, *_: (p, 0, 0)),
            scratch_shapes=[pltpu.VMEM((block_count, size, tile_size), jnp.bfloat16)],
        ),
        cost_estimate=pl.CostEstimate(
            flops=2 * peers * use_count * tile_size * tile_size * size,
            bytes_accessed=2 * (tiles.size + blocks.size + peers * height * tile_size),
            transcendentals=0,
        ),
        name="apply_tiles",
    )(rows, counts, cols, tiles, blocks)


def join_kernel(gram_blocks, start, spot_ref, cols_ref, phi_ref, sent_ref, keep_ref, give_ref, total):
    step = pl.program_id(0)
    height, features = total.shape
    peers = sent_ref.shape[0]

    @pl.when(step == 0)
    def _():
        own = [phi_ref[spot_ref[0] * gram_blocks + b] for b in range(gram_blocks)]
        tall = jnp.concatenate(own, axis=0)
        part = tall[:, start : start + height]
        total[...] = lax.dot_general(
            part, tall, (((0,), (0,)), ((), ())), preferred_element_type=jnp.float32
        )

    left = jnp.concatenate([sent_ref[s, :height] for s in range(peers)], axis=1)
    right = jnp.concatenate([phi_ref[cols_ref[step * peers + s]] for s in range(peers)], axis=0)
    total[...] += dot(left, right)

    @pl.when(step == pl.num_programs(0) - 1)
    def _():
        rows = total[...].reshape(height // 16, 2, 8, features)
        even, odd = rows[:, 0], rows[:, 1]
        place = lax.broadcasted_iota(jnp.int32, even.shape, 1)
        lower = lax.rem(place, 4) < 2
        zero = jnp.where(lower, even, jnp.roll(odd, 2, axis=1))
        one = jnp.where(lower, jnp.roll(even, -2, axis=1), odd)
        own_one = spot_ref[1] == 1
        keep_ref[...] = jnp.where(own_one, one, zero)
        give_ref[...] = jnp.where(own_one, zero, one)


def join(spot, cols, blocks, sent, gram_blocks, start, size):
    peers, height, tile_size = sent.shape
    block_count, _, features = blocks.shape
    per_step = 8
    half = jax.ShapeDtypeStruct((size // 16, 8, features), jnp.float32)
    return pl.pallas_call(
        functools.partial(join_kernel, gram_blocks, start),
        out_shape=(half, half),
        grid_spec=pltpu.PrefetchScalarGridSpec(
            num_scalar_prefetch=2,
            grid=(peers // per_step,),
            in_specs=[
                pl.BlockSpec((block_count, tile_size, features), lambda p, *_: (0, 0, 0)),
                pl.BlockSpec((per_step, height, tile_size), lambda p, *_: (p, 0, 0)),
            ],
            out_specs=[
                pl.BlockSpec((size // 16, 8, features), lambda p, *_: (0, 0, 0)),
                pl.BlockSpec((size // 16, 8, features), lambda p, *_: (0, 0, 0)),
            ],
            scratch_shapes=[pltpu.VMEM((size, features), jnp.float32)],
        ),
        compiler_params=pltpu.CompilerParams(vmem_limit_bytes=24 << 20),
        cost_estimate=pl.CostEstimate(
            flops=2 * peers * tile_size * size * features,
            bytes_accessed=2 * (blocks.size + sent.size) + 8 * size * features,
            transcendentals=0,
        ),
        name="join",
    )(spot, cols, blocks, sent)


def body(basis_rows, tile_blocks, tile_cols, tile_rows, tile_counts):
    shards = lax.axis_size("state")
    groups = lax.axis_size("group")
    local_rows, features = basis_rows.shape
    tile_size = tile_blocks.shape[-1]
    block_count = local_rows // tile_size
    blocks = basis_rows.reshape(block_count, tile_size, features)
    exchange = functools.partial(
        lax.all_to_all, axis_name="state", split_axis=0, concat_axis=0, tiled=True
    )
    swap = [(g, g ^ 1) for g in range(groups)]
    member = lax.axis_index("group")
    spot = jnp.stack([member, member & 1]).astype(jnp.int32)

    rows = tile_rows[0, 0].reshape(-1)
    counts = tile_counts[0, 0]
    cols = tile_cols[0, 0]
    tiles = tile_blocks[0, 0]
    rest = features - first_features
    gram_blocks = block_count // groups

    sent = apply_tiles(rows, counts, cols, tiles, blocks, 0, first_features, True)
    got_one = exchange(sent)
    sent = apply_tiles(rows, counts, cols, tiles, blocks, first_features, rest, False)
    got_two = exchange(sent)
    wanted = got_one[:, first_features, 0].astype(jnp.int32)
    keep_one, give_one = join(spot, wanted, blocks, got_one, gram_blocks, 0, first_features)
    keep_two, give_two = join(spot, wanted, blocks, got_two, gram_blocks, first_features, rest)
    half = jnp.concatenate(
        [
            keep_one + lax.ppermute(give_one, "group", swap),
            keep_two + lax.ppermute(give_two, "group", swap),
        ],
        axis=0,
    )
    owned = exchange(half).sum(0)

    quads = groups // 2
    quad = member >> 1
    final = lax.dynamic_slice_in_dim(owned, 2 * place_of(quad), 2, 0)
    for shift in range(1, quads):
        target = lax.rem(quad + shift, quads)
        piece = lax.dynamic_slice_in_dim(owned, 2 * place_of(target), 2, 0)
        ring = [(g, (g + 2 * shift) % groups) for g in range(groups)]
        final = final + lax.ppermute(piece, "group", ring)
    return final * (1.0 / math.sqrt(local_rows * shards))


def place_of(quad):
    return (quad & 1) * 2 + (quad >> 1)


def solution(mesh):
    in_specs = (
        P("state", None),
        P("state", "group", None, None, None, None),
        P("state", "group", None),
        P("state", "group", None, None),
        P("state", "group", None),
    )
    out_specs = P(("state", "group"), None)
    return jax.shard_map(body, mesh=mesh, in_specs=in_specs, out_specs=out_specs, check_vma=False)
```

```python
import functools
import math

import jax
import jax.numpy as jnp
from jax import lax
from jax.experimental import pallas as pl
from jax.experimental.pallas import tpu as pltpu
from jax.sharding import PartitionSpec as P


discount = 0.95
extra_rows = 16
peers_per_step = 8


def dot(left, right):
    return jnp.dot(left, right, preferred_element_type=jnp.float32)


def apply_kernel(rows_ref, counts_ref, cols_ref, tiles_ref, phi_ref, out_ref, turned):
    step = pl.program_id(0)
    block_count, features, _ = turned.shape
    peers, use_count = tiles_ref.shape[:2]

    @pl.when(step == 0)
    def _():
        def turn(b, carry):
            for k in range(2):
                turned[2 * b + k] = phi_ref[2 * b + k].T
            return carry

        lax.fori_loop(0, block_count // 2, turn, 0)

    for local in range(peers):
        peer = step * peers + local
        count = counts_ref[peer]
        left = jnp.concatenate([turned[rows_ref[u, peer]] for u in range(use_count)], axis=1)
        right = jnp.concatenate(
            [
                jnp.where(u < count, tiles_ref[local, u], jnp.zeros((), tiles_ref.dtype))
                for u in range(use_count)
            ],
            axis=0,
        )
        product = dot(left, right) * (-discount)
        out_ref[local, :features] = product.astype(out_ref.dtype)
        column = jnp.full((extra_rows, out_ref.shape[2]), cols_ref[peer], jnp.int32)
        out_ref[local, features:] = column.astype(jnp.float32).astype(out_ref.dtype)


def apply_tiles(rows, counts, cols, tiles, blocks):
    peers, use_count, tile_size, _ = tiles.shape
    block_count, _, features = blocks.shape
    height = features + extra_rows
    per_step = peers_per_step
    return pl.pallas_call(
        apply_kernel,
        out_shape=jax.ShapeDtypeStruct((peers, height, tile_size), jnp.bfloat16),
        grid_spec=pltpu.PrefetchScalarGridSpec(
            num_scalar_prefetch=3,
            grid=(peers // per_step,),
            in_specs=[
                pl.BlockSpec(
                    (per_step, use_count, tile_size, tile_size), lambda p, *_: (p, 0, 0, 0)
                ),
                pl.BlockSpec((block_count, tile_size, features), lambda p, *_: (0, 0, 0)),
            ],
            out_specs=pl.BlockSpec((per_step, height, tile_size), lambda p, *_: (p, 0, 0)),
            scratch_shapes=[pltpu.VMEM((block_count, features, tile_size), jnp.bfloat16)],
        ),
        cost_estimate=pl.CostEstimate(
            flops=2 * peers * use_count * tile_size * tile_size * features,
            bytes_accessed=2 * (tiles.size + blocks.size + peers * height * tile_size),
            transcendentals=0,
        ),
        name="apply_tiles",
    )(rows, counts, cols, tiles, blocks)


def halves(total, own_one):
    height, features = total.shape
    rows = total.reshape(height // 16, 2, 8, features)
    even, odd = rows[:, 0], rows[:, 1]
    place = lax.broadcasted_iota(jnp.int32, even.shape, 1)
    lower = lax.rem(place, 4) < 2
    zero = jnp.where(lower, even, jnp.roll(odd, 2, axis=1))
    one = jnp.where(lower, jnp.roll(even, -2, axis=1), odd)
    return jnp.where(own_one, one, zero), jnp.where(own_one, zero, one)


def gram_kernel(spot_ref, phi_ref, out_ref):
    depth, tile_size, features = phi_ref.shape
    tall = phi_ref[...].reshape(depth * tile_size, features)
    total = lax.dot_general(
        tall, tall, (((0,), (0,)), ((), ())), preferred_element_type=jnp.float32
    )
    out_ref[...] = halves(total, spot_ref[1] == 1)[0]


def gram_rows(spot, blocks, depth):
    _, tile_size, features = blocks.shape
    return pl.pallas_call(
        gram_kernel,
        out_shape=jax.ShapeDtypeStruct((features // 16, 8, features), jnp.float32),
        grid_spec=pltpu.PrefetchScalarGridSpec(
            num_scalar_prefetch=1,
            grid=(1,),
            in_specs=[
                pl.BlockSpec((depth, tile_size, features), lambda p, spot_ref: (spot_ref[0], 0, 0))
            ],
            out_specs=pl.BlockSpec((features // 16, 8, features), lambda p, *_: (0, 0, 0)),
        ),
        compiler_params=pltpu.CompilerParams(vmem_limit_bytes=16 << 20),
        cost_estimate=pl.CostEstimate(
            flops=2 * depth * tile_size * features * features,
            bytes_accessed=2 * depth * tile_size * features + 2 * features * features,
            transcendentals=0,
        ),
        name="gram_rows",
    )(spot, blocks)


def join_kernel(spot_ref, phi_ref, sent_ref, keep_ref, give_ref, total):
    step = pl.program_id(0)
    height, _ = total.shape
    peers = sent_ref.shape[0]

    @pl.when(step == 0)
    def _():
        total[...] = jnp.zeros_like(total)

    wanted = [
        jnp.max(sent_ref[s, height:].astype(jnp.float32)).astype(jnp.int32) for s in range(peers)
    ]
    left = jnp.concatenate([sent_ref[s, :height] for s in range(peers)], axis=1)
    right = jnp.concatenate([phi_ref[w] for w in wanted], axis=0)
    total[...] += dot(left, right)

    @pl.when(step == pl.num_programs(0) - 1)
    def _():
        keep, give = halves(total[...], spot_ref[1] == 1)
        keep_ref[...] = keep
        give_ref[...] = give


def join(spot, blocks, sent, per_step=8):
    peers, height, tile_size = sent.shape
    block_count, _, features = blocks.shape
    half = jax.ShapeDtypeStruct((features // 16, 8, features), jnp.float32)
    return pl.pallas_call(
        join_kernel,
        out_shape=(half, half),
        grid_spec=pltpu.PrefetchScalarGridSpec(
            num_scalar_prefetch=1,
            grid=(peers // per_step,),
            in_specs=[
                pl.BlockSpec((block_count, tile_size, features), lambda p, *_: (0, 0, 0)),
                pl.BlockSpec((per_step, height, tile_size), lambda p, *_: (p, 0, 0)),
            ],
            out_specs=[
                pl.BlockSpec((features // 16, 8, features), lambda p, *_: (0, 0, 0)),
                pl.BlockSpec((features // 16, 8, features), lambda p, *_: (0, 0, 0)),
            ],
            scratch_shapes=[pltpu.VMEM((features, features), jnp.float32)],
        ),
        compiler_params=pltpu.CompilerParams(vmem_limit_bytes=24 << 20),
        cost_estimate=pl.CostEstimate(
            flops=2 * peers * tile_size * features * features,
            bytes_accessed=2 * (blocks.size + sent.size) + 8 * features * features,
            transcendentals=0,
        ),
        name="join",
    )(spot, blocks, sent)


def body(basis_rows, tile_blocks, tile_cols, tile_rows, tile_counts):
    shards = lax.axis_size("state")
    groups = lax.axis_size("group")
    local_rows, features = basis_rows.shape
    tile_size = tile_blocks.shape[-1]
    block_count = local_rows // tile_size
    blocks = basis_rows.reshape(block_count, tile_size, features)
    exchange = functools.partial(
        lax.all_to_all, axis_name="state", split_axis=0, concat_axis=0, tiled=True
    )
    swap = [(g, g ^ 1) for g in range(groups)]
    member = lax.axis_index("group")
    spot = jnp.stack([member >> 1, member & 1]).astype(jnp.int32)

    sent = apply_tiles(
        tile_rows[0, 0].T, tile_counts[0, 0], tile_cols[0, 0], tile_blocks[0, 0], blocks
    )
    got = exchange(sent)
    gram = gram_rows(spot, blocks, 2 * block_count // groups)
    keep, give = join(spot, blocks, got)
    half = (keep + gram) + lax.ppermute(give, "group", swap)
    owned = exchange(half).sum(0)

    quads = groups // 2
    quad = member >> 1
    final = lax.dynamic_slice_in_dim(owned, 2 * place_of(quad), 2, 0)
    for shift in range(1, quads):
        target = lax.rem(quad + shift, quads)
        piece = lax.dynamic_slice_in_dim(owned, 2 * place_of(target), 2, 0)
        ring = [(g, (g + 2 * shift) % groups) for g in range(groups)]
        final = final + lax.ppermute(piece, "group", ring)
    return final * (1.0 / math.sqrt(local_rows * shards))


def place_of(quad):
    return (quad & 1) * 2 + (quad >> 1)


def solution(mesh):
    in_specs = (
        P("state", None),
        P("state", "group", None, None, None, None),
        P("state", "group", None),
        P("state", "group", None, None),
        P("state", "group", None),
    )
    out_specs = P(("state", "group"), None)
    return jax.shard_map(body, mesh=mesh, in_specs=in_specs, out_specs=out_specs, check_vma=False)
```

```python
import functools
import math

import jax
import jax.numpy as jnp
from jax import lax
from jax.experimental import pallas as pl
from jax.experimental.pallas import tpu as pltpu
from jax.sharding import PartitionSpec as P


discount = 0.95
extra_rows = 8
peers_per_step = 8


def dot(left, right):
    return jnp.dot(left, right, preferred_element_type=jnp.float32)


def apply_kernel(rows_ref, counts_ref, cols_ref, tiles_ref, phi_ref, out_ref):
    step = pl.program_id(0)
    peers, use_count, tile_size, _ = tiles_ref.shape
    features = phi_ref.shape[2]
    for local in range(peers):
        peer = step * peers + local
        count = counts_ref[peer]
        left = jnp.concatenate(
            [
                jnp.where(u < count, tiles_ref[local, u], jnp.zeros((), tiles_ref.dtype)).T
                for u in range(use_count)
            ],
            axis=1,
        )
        right = jnp.concatenate([phi_ref[rows_ref[u, 0, peer]] for u in range(use_count)], axis=0)
        product = (dot(left, right) * (-discount)).astype(out_ref.dtype)
        for part in range(features // tile_size):
            span = pl.ds(part * tile_size, tile_size)
            out_ref[local, span] = product[:, part * tile_size : (part + 1) * tile_size]
        column = jnp.full((extra_rows, out_ref.shape[2]), cols_ref[peer], jnp.int32)
        out_ref[local, features:] = column.astype(jnp.float32).astype(out_ref.dtype)


def apply_tiles(rows, counts, cols, tiles, blocks):
    peers, use_count, tile_size, _ = tiles.shape
    block_count, _, features = blocks.shape
    height = features + extra_rows
    per_step = peers_per_step
    return pl.pallas_call(
        apply_kernel,
        out_shape=jax.ShapeDtypeStruct((peers, height, tile_size), jnp.bfloat16),
        grid_spec=pltpu.PrefetchScalarGridSpec(
            num_scalar_prefetch=3,
            grid=(peers // per_step,),
            in_specs=[
                pl.BlockSpec(
                    (per_step, use_count, tile_size, tile_size), lambda p, *_: (p, 0, 0, 0)
                ),
                pl.BlockSpec((block_count, tile_size, features), lambda p, *_: (0, 0, 0)),
            ],
            out_specs=pl.BlockSpec((per_step, height, tile_size), lambda p, *_: (p, 0, 0)),
        ),
        cost_estimate=pl.CostEstimate(
            flops=2 * peers * use_count * tile_size * tile_size * features,
            bytes_accessed=2 * (tiles.size + blocks.size + peers * height * tile_size),
            transcendentals=0,
        ),
        name="apply_tiles",
    )(rows, counts, cols, tiles, blocks)


def halves(total, own_one):
    height, features = total.shape
    rows = total.reshape(height // 16, 2, 8, features)
    even, odd = rows[:, 0], rows[:, 1]
    place = lax.broadcasted_iota(jnp.int32, even.shape, 1)
    lower = lax.rem(place, 4) < 2
    zero = jnp.where(lower, even, jnp.roll(odd, 2, axis=1))
    one = jnp.where(lower, jnp.roll(even, -2, axis=1), odd)
    return jnp.where(own_one, one, zero), jnp.where(own_one, zero, one)


def gram_kernel(spot_ref, phi_ref, out_ref):
    depth, tile_size, features = phi_ref.shape
    tall = phi_ref[...].reshape(depth * tile_size, features)
    total = lax.dot_general(
        tall, tall, (((0,), (0,)), ((), ())), preferred_element_type=jnp.float32
    )
    out_ref[...] = halves(total, spot_ref[1] == 1)[0]


def gram_rows(spot, blocks, depth):
    _, tile_size, features = blocks.shape
    return pl.pallas_call(
        gram_kernel,
        out_shape=jax.ShapeDtypeStruct((features // 16, 8, features), jnp.float32),
        grid_spec=pltpu.PrefetchScalarGridSpec(
            num_scalar_prefetch=1,
            grid=(1,),
            in_specs=[
                pl.BlockSpec((depth, tile_size, features), lambda p, spot_ref: (spot_ref[0], 0, 0))
            ],
            out_specs=pl.BlockSpec((features // 16, 8, features), lambda p, *_: (0, 0, 0)),
        ),
        compiler_params=pltpu.CompilerParams(vmem_limit_bytes=16 << 20),
        cost_estimate=pl.CostEstimate(
            flops=2 * depth * tile_size * features * features,
            bytes_accessed=2 * depth * tile_size * features + 2 * features * features,
            transcendentals=0,
        ),
        name="gram_rows",
    )(spot, blocks)


def join_kernel(spot_ref, phi_ref, sent_ref, keep_ref, give_ref, total):
    step = pl.program_id(0)
    height, _ = total.shape
    peers = sent_ref.shape[0]

    @pl.when(step == 0)
    def _():
        total[...] = jnp.zeros_like(total)

    wanted = [
        jnp.max(sent_ref[s, height:].astype(jnp.float32)).astype(jnp.int32) for s in range(peers)
    ]
    tile_size = sent_ref.shape[2]
    left = jnp.concatenate(
        [
            jnp.concatenate(
                [
                    sent_ref[s, pl.ds(part * tile_size, tile_size)].T
                    for part in range(height // tile_size)
                ],
                axis=0,
            )
            for s in range(peers)
        ],
        axis=1,
    )
    right = jnp.concatenate([phi_ref[w] for w in wanted], axis=0)
    total[...] += dot(left, right)

    @pl.when(step == pl.num_programs(0) - 1)
    def _():
        keep, give = halves(total[...], spot_ref[1] == 1)
        keep_ref[...] = keep
        give_ref[...] = give


def join(spot, blocks, sent, per_step=8):
    peers, height, tile_size = sent.shape
    block_count, _, features = blocks.shape
    half = jax.ShapeDtypeStruct((features // 16, 8, features), jnp.float32)
    return pl.pallas_call(
        join_kernel,
        out_shape=(half, half),
        grid_spec=pltpu.PrefetchScalarGridSpec(
            num_scalar_prefetch=1,
            grid=(peers // per_step,),
            in_specs=[
                pl.BlockSpec((block_count, tile_size, features), lambda p, *_: (0, 0, 0)),
                pl.BlockSpec((per_step, height, tile_size), lambda p, *_: (p, 0, 0)),
            ],
            out_specs=[
                pl.BlockSpec((features // 16, 8, features), lambda p, *_: (0, 0, 0)),
                pl.BlockSpec((features // 16, 8, features), lambda p, *_: (0, 0, 0)),
            ],
            scratch_shapes=[pltpu.VMEM((features, features), jnp.float32)],
        ),
        compiler_params=pltpu.CompilerParams(vmem_limit_bytes=24 << 20),
        cost_estimate=pl.CostEstimate(
            flops=2 * peers * tile_size * features * features,
            bytes_accessed=2 * (blocks.size + sent.size) + 8 * features * features,
            transcendentals=0,
        ),
        name="join",
    )(spot, blocks, sent)


def body(basis_rows, tile_blocks, tile_cols, tile_rows, tile_counts):
    shards = lax.axis_size("state")
    quads = lax.axis_size("quad")
    local_rows, features = basis_rows.shape
    tile_size = tile_blocks.shape[-1]
    block_count = local_rows // tile_size
    blocks = basis_rows.reshape(block_count, tile_size, features)
    exchange = functools.partial(
        lax.all_to_all, axis_name="state", split_axis=0, concat_axis=0, tiled=True
    )
    spot = jnp.stack([lax.axis_index("quad"), lax.axis_index("core")]).astype(jnp.int32)

    sent = apply_tiles(
        tile_rows[0].transpose(2, 0, 1),
        tile_counts[0, 0],
        tile_cols[0, 0],
        tile_blocks[0, 0],
        blocks,
    )
    quad = lax.axis_index("quad")
    starts = [2 * place_of(lax.rem(quad + shift, quads)) for shift in range(quads)]
    sent, spot, starts = lax.optimization_barrier((sent, spot, starts))
    got = exchange(sent)
    keep, give = join(spot, blocks, got)
    taken = lax.ppermute(give, "core", [(0, 1), (1, 0)])
    gram = gram_rows(spot, blocks, block_count // quads)
    owned = exchange((keep + gram) + taken).sum(0)

    pieces = [lax.dynamic_slice_in_dim(owned, start, 2, 0) for start in starts]
    final = pieces[0]
    for shift in range(1, quads):
        ring = [(q, (q + shift) % quads) for q in range(quads)]
        final = final + lax.ppermute(pieces[shift], "quad", ring)
    return final * (1.0 / math.sqrt(local_rows * shards))


def place_of(quad):
    return (quad & 1) * 2 + (quad >> 1)


def solution(mesh):
    shards, groups = mesh.devices.shape
    fine = jax.sharding.Mesh(
        mesh.devices.reshape(shards, groups // 2, 2), ("state", "quad", "core")
    )
    group = ("quad", "core")
    in_specs = (
        P("state", None),
        P("state", group, None, None, None, None),
        P("state", group, None),
        P("state", group, None, None),
        P("state", group, None),
    )
    out_specs = P(("state",) + group, None)
    return jax.shard_map(body, mesh=fine, in_specs=in_specs, out_specs=out_specs, check_vma=False)
```

```python
import functools
import math

import jax
import jax.numpy as jnp
from jax import lax
from jax.experimental import pallas as pl
from jax.experimental.pallas import tpu as pltpu
from jax.sharding import PartitionSpec as P


discount = 0.95
extra_rows = 8
peers_per_step = 16
peers_per_dot = 8


def dot(left, right):
    return jnp.dot(left, right, preferred_element_type=jnp.float32)


def apply_kernel(rows_ref, counts_ref, cols_ref, tiles_ref, phi_ref, out_ref):
    step = pl.program_id(0)
    peers, use_count, tile_size, _ = tiles_ref.shape
    features = phi_ref.shape[2]
    for local in range(peers):
        peer = step * peers + local
        count = counts_ref[peer]
        left = jnp.concatenate(
            [
                jnp.where(u < count, tiles_ref[local, u], jnp.zeros((), tiles_ref.dtype)).T
                for u in range(use_count)
            ],
            axis=1,
        )
        right = jnp.concatenate([phi_ref[rows_ref[u, 0, peer]] for u in range(use_count)], axis=0)
        product = (dot(left, right) * (-discount)).astype(out_ref.dtype)
        for part in range(features // tile_size):
            span = pl.ds(part * tile_size, tile_size)
            out_ref[local, span] = product[:, part * tile_size : (part + 1) * tile_size]
        column = jnp.full((extra_rows, out_ref.shape[2]), cols_ref[peer], jnp.int32)
        out_ref[local, features:] = column.astype(jnp.float32).astype(out_ref.dtype)


def apply_tiles(rows, counts, cols, tiles, blocks):
    peers, use_count, tile_size, _ = tiles.shape
    block_count, _, features = blocks.shape
    height = features + extra_rows
    per_step = peers_per_step
    return pl.pallas_call(
        apply_kernel,
        out_shape=jax.ShapeDtypeStruct((peers, height, tile_size), jnp.bfloat16),
        grid_spec=pltpu.PrefetchScalarGridSpec(
            num_scalar_prefetch=3,
            grid=(peers // per_step,),
            in_specs=[
                pl.BlockSpec(
                    (per_step, use_count, tile_size, tile_size), lambda p, *_: (p, 0, 0, 0)
                ),
                pl.BlockSpec((block_count, tile_size, features), lambda p, *_: (0, 0, 0)),
            ],
            out_specs=pl.BlockSpec((per_step, height, tile_size), lambda p, *_: (p, 0, 0)),
        ),
        cost_estimate=pl.CostEstimate(
            flops=2 * peers * use_count * tile_size * tile_size * features,
            bytes_accessed=2 * (tiles.size + blocks.size + peers * height * tile_size),
            transcendentals=0,
        ),
        name="apply_tiles",
    )(rows, counts, cols, tiles, blocks)


def store_half(total_ref, core, out_ref):
    parts, height, _ = total_ref.shape
    for k in range(2):
        for part in range(parts):
            rows = total_ref[part, pl.ds(core * 2 + k, height // 4, stride=4), :]
            out_ref[pl.ds(k * parts + part, height // 4, stride=2 * parts), :] = rows


def gram_kernel(spot_ref, phi_ref, out_ref, total):
    depth, tile_size, features = phi_ref.shape
    tall = phi_ref[...].reshape(depth * tile_size, features)
    product = lax.dot_general(
        tall, tall, (((0,), (0,)), ((), ())), preferred_element_type=jnp.float32
    )
    parts, _, lanes = total.shape
    for part in range(parts):
        total[part] = product[:, part * lanes : (part + 1) * lanes]
    store_half(total, spot_ref[1], out_ref)


def gram_rows(spot, blocks, depth):
    _, tile_size, features = blocks.shape
    return pl.pallas_call(
        gram_kernel,
        out_shape=jax.ShapeDtypeStruct((features * features // 256, 128), jnp.float32),
        grid_spec=pltpu.PrefetchScalarGridSpec(
            num_scalar_prefetch=1,
            grid=(1,),
            in_specs=[
                pl.BlockSpec((depth, tile_size, features), lambda p, spot_ref: (spot_ref[0], 0, 0))
            ],
            out_specs=pl.BlockSpec((features * features // 256, 128), lambda p, *_: (0, 0)),
            scratch_shapes=[pltpu.VMEM((features // 128, features, 128), jnp.float32)],
        ),
        compiler_params=pltpu.CompilerParams(vmem_limit_bytes=16 << 20),
        cost_estimate=pl.CostEstimate(
            flops=2 * depth * tile_size * features * features,
            bytes_accessed=2 * depth * tile_size * features + 2 * features * features,
            transcendentals=0,
        ),
        name="gram_rows",
    )(spot, blocks)


def join_kernel(spot_ref, phi_ref, sent_ref, keep_ref, give_ref, total):
    parts, height, lanes = total.shape
    peers = sent_ref.shape[0]
    wanted = [
        jnp.max(sent_ref[s, height:].astype(jnp.float32)).astype(jnp.int32) for s in range(peers)
    ]
    for first in range(0, peers, peers_per_dot):
        group = range(first, first + peers_per_dot)
        left = jnp.concatenate(
            [
                jnp.concatenate(
                    [sent_ref[s, pl.ds(part * lanes, lanes)].T for part in range(parts)], axis=0
                )
                for s in group
            ],
            axis=1,
        )
        right = jnp.concatenate([phi_ref[wanted[s]] for s in group], axis=0)
        product = dot(left, right)
        for part in range(parts):
            piece = product[:, part * lanes : (part + 1) * lanes]
            total[part] = piece if first == 0 else total[part] + piece
    store_half(total, spot_ref[1], keep_ref)
    store_half(total, 1 - spot_ref[1], give_ref)


def join(spot, blocks, sent):
    peers, _, tile_size = sent.shape
    _, _, features = blocks.shape
    half = jax.ShapeDtypeStruct((features * features // 256, 128), jnp.float32)
    whole = pl.BlockSpec(memory_space=pltpu.VMEM)
    return pl.pallas_call(
        join_kernel,
        out_shape=(half, half),
        in_specs=[pl.BlockSpec(memory_space=pltpu.SMEM), whole, whole],
        out_specs=[whole, whole],
        scratch_shapes=[pltpu.VMEM((features // 128, features, 128), jnp.float32)],
        compiler_params=pltpu.CompilerParams(vmem_limit_bytes=24 << 20),
        cost_estimate=pl.CostEstimate(
            flops=2 * peers * tile_size * features * features,
            bytes_accessed=2 * (blocks.size + sent.size) + 8 * features * features,
            transcendentals=0,
        ),
        name="join",
    )(spot, blocks, sent)


def body(basis_rows, tile_blocks, tile_cols, tile_rows, tile_counts):
    shards = lax.axis_size(("xy", "zl"))
    quads = lax.axis_size("quad")
    local_rows, features = basis_rows.shape
    tile_size = tile_blocks.shape[-1]
    block_count = local_rows // tile_size
    blocks = basis_rows.reshape(block_count, tile_size, features)
    exchange = functools.partial(
        lax.all_to_all, split_axis=0, concat_axis=0, tiled=True
    )
    spot = jnp.stack([lax.axis_index("quad"), lax.axis_index("core")]).astype(jnp.int32)

    sent = apply_tiles(
        tile_rows[0].transpose(2, 0, 1),
        tile_counts[0, 0],
        tile_cols[0, 0],
        tile_blocks[0, 0],
        blocks,
    )
    sent, spot = lax.optimization_barrier((sent, spot))
    got = exchange(sent, ("xy", "zl"))
    keep, give = join(spot, blocks, got)
    taken = lax.ppermute(give, "core", [(0, 1), (1, 0)])
    gram = gram_rows(spot, blocks, block_count // quads)
    half = ((keep + gram) + taken).reshape(shards // 2, -1, tile_size)
    owned = exchange(half, "xy").sum(0)
    owned = exchange(owned.reshape(2 * quads, -1, tile_size), ("zl", "quad")).sum(0)
    return owned.reshape(-1, features) * (1.0 / math.sqrt(local_rows * shards))


def solution(mesh):
    shards, groups = mesh.devices.shape
    fine = jax.sharding.Mesh(
        mesh.devices.reshape(shards // 2, 2, groups // 2, 2), ("xy", "zl", "quad", "core")
    )
    group = ("quad", "core")
    in_specs = (
        P(("xy","zl"), None),
        P(("xy","zl"), group, None, None, None, None),
        P(("xy","zl"), group, None),
        P(("xy","zl"), group, None, None),
        P(("xy","zl"), group, None),
    )
    out_specs = P(("xy","zl") + group, None)
    return jax.shard_map(body, mesh=fine, in_specs=in_specs, out_specs=out_specs, check_vma=False)
```

```python
import functools
import math

import jax
import jax.numpy as jnp
from jax import lax
from jax.experimental import pallas as pl
from jax.experimental.pallas import tpu as pltpu
from jax.sharding import PartitionSpec as P


discount = 0.95
extra_rows = 8
tile_groups = 4
peers_per_dot = 8


def dot(left, right):
    return jnp.dot(left, right, preferred_element_type=jnp.float32)


def apply_kernel(
    rows_ref, counts_ref, cols_ref, tiles_hbm, phi_hbm, out, tiles, phi, tile_sems, phi_sem
):
    peers, use_count, tile_size, _ = tiles.shape
    features = phi.shape[2]
    groups = tile_sems.shape[0]
    size = peers // groups
    spans = [pl.ds(i * size, size) for i in range(groups)]
    load_phi = pltpu.make_async_copy(phi_hbm, phi, phi_sem)
    loads = [
        pltpu.make_async_copy(tiles_hbm.at[spans[i]], tiles.at[spans[i]], tile_sems.at[i])
        for i in range(groups)
    ]
    load_phi.start()
    loads[0].start()
    loads[1].start()
    load_phi.wait()
    for i in range(2, groups):
        loads[i].start()
    for i in range(groups):
        loads[i].wait()
        for peer in range(i * size, (i + 1) * size):
            count = counts_ref[peer]
            left = jnp.concatenate(
                [
                    jnp.where(u < count, tiles[peer, u], jnp.zeros((), tiles.dtype)).T
                    for u in range(use_count)
                ],
                axis=1,
            )
            right = jnp.concatenate([phi[rows_ref[u, 0, peer]] for u in range(use_count)], axis=0)
            product = (dot(left, right) * (-discount)).astype(out.dtype)
            for part in range(features // tile_size):
                span = pl.ds(part * tile_size, tile_size)
                out[peer, span] = product[:, part * tile_size : (part + 1) * tile_size]
            column = jnp.full((extra_rows, tile_size), cols_ref[peer], jnp.int32)
            out[peer, features:] = column.astype(jnp.float32).astype(out.dtype)


def apply_tiles(rows, counts, cols, tiles, blocks):
    peers, use_count, tile_size, _ = tiles.shape
    _, _, features = blocks.shape
    result = jax.ShapeDtypeStruct((peers, features + extra_rows, tile_size), jnp.bfloat16)
    there = pl.BlockSpec(memory_space=pl.ANY)
    return pl.pallas_call(
        apply_kernel,
        out_shape=result,
        grid_spec=pltpu.PrefetchScalarGridSpec(
            num_scalar_prefetch=3,
            grid=(1,),
            in_specs=[there, there],
            out_specs=pl.BlockSpec(memory_space=pltpu.VMEM),
            scratch_shapes=[
                pltpu.VMEM(tiles.shape, tiles.dtype),
                pltpu.VMEM(blocks.shape, blocks.dtype),
                pltpu.SemaphoreType.DMA((tile_groups,)),
                pltpu.SemaphoreType.DMA,
            ],
        ),
        compiler_params=pltpu.CompilerParams(vmem_limit_bytes=24 << 20),
        cost_estimate=pl.CostEstimate(
            flops=2 * peers * use_count * tile_size * tile_size * features,
            bytes_accessed=2 * (tiles.size + blocks.size + result.size),
            transcendentals=0,
        ),
        name="apply_tiles",
    )(
        *[
            pltpu.with_memory_space_constraint(array, pltpu.HBM)
            for array in (rows, counts, cols, tiles, blocks)
        ]
    )


def store_half(total_ref, core, out_ref):
    parts, height, _ = total_ref.shape
    for k in range(2):
        for part in range(parts):
            rows = total_ref[part, pl.ds(core * 2 + k, height // 4, stride=4), :]
            out_ref[pl.ds(2 * part + k, height // 4, stride=2 * parts), :] = rows


def gram_kernel(spot_ref, phi_ref, out_ref, total):
    depth, tile_size, features = phi_ref.shape
    tall = phi_ref[...].reshape(depth * tile_size, features)
    product = lax.dot_general(
        tall, tall, (((0,), (0,)), ((), ())), preferred_element_type=jnp.float32
    )
    parts, _, lanes = total.shape
    for part in range(parts):
        total[part] = product[:, part * lanes : (part + 1) * lanes]
    store_half(total, spot_ref[1], out_ref)


def gram_rows(spot, blocks, depth):
    _, tile_size, features = blocks.shape
    return pl.pallas_call(
        gram_kernel,
        out_shape=jax.ShapeDtypeStruct((features * features // 256, 128), jnp.float32),
        grid_spec=pltpu.PrefetchScalarGridSpec(
            num_scalar_prefetch=1,
            grid=(1,),
            in_specs=[
                pl.BlockSpec((depth, tile_size, features), lambda p, spot_ref: (spot_ref[0], 0, 0))
            ],
            out_specs=pl.BlockSpec((features * features // 256, 128), lambda p, *_: (0, 0)),
            scratch_shapes=[pltpu.VMEM((features // 128, features, 128), jnp.float32)],
        ),
        compiler_params=pltpu.CompilerParams(vmem_limit_bytes=16 << 20),
        cost_estimate=pl.CostEstimate(
            flops=2 * depth * tile_size * features * features,
            bytes_accessed=2 * depth * tile_size * features + 2 * features * features,
            transcendentals=0,
        ),
        name="gram_rows",
    )(spot, blocks)


def join_kernel(spot_ref, phi_ref, sent_ref, keep_ref, give_ref, total):
    parts, height, lanes = total.shape
    peers = sent_ref.shape[0]
    wanted = [
        jnp.max(sent_ref[s, height:].astype(jnp.float32)).astype(jnp.int32) for s in range(peers)
    ]
    for first in range(0, peers, peers_per_dot):
        group = range(first, first + peers_per_dot)
        left = jnp.concatenate(
            [
                jnp.concatenate(
                    [sent_ref[s, pl.ds(part * lanes, lanes)].T for part in range(parts)], axis=0
                )
                for s in group
            ],
            axis=1,
        )
        right = jnp.concatenate([phi_ref[wanted[s]] for s in group], axis=0)
        product = dot(left, right)
        for part in range(parts):
            piece = product[:, part * lanes : (part + 1) * lanes]
            total[part] = piece if first == 0 else total[part] + piece
    store_half(total, spot_ref[1], keep_ref)
    store_half(total, 1 - spot_ref[1], give_ref)


def join(spot, blocks, sent):
    peers, _, tile_size = sent.shape
    _, _, features = blocks.shape
    half = jax.ShapeDtypeStruct((features * features // 256, 128), jnp.float32)
    whole = pl.BlockSpec(memory_space=pltpu.VMEM)
    return pl.pallas_call(
        join_kernel,
        out_shape=(half, half),
        in_specs=[pl.BlockSpec(memory_space=pltpu.SMEM), whole, whole],
        out_specs=[whole, whole],
        scratch_shapes=[pltpu.VMEM((features // 128, features, 128), jnp.float32)],
        compiler_params=pltpu.CompilerParams(vmem_limit_bytes=24 << 20),
        cost_estimate=pl.CostEstimate(
            flops=2 * peers * tile_size * features * features,
            bytes_accessed=2 * (blocks.size + sent.size) + 8 * features * features,
            transcendentals=0,
        ),
        name="join",
    )(spot, blocks, sent)


def body(basis_rows, tile_blocks, tile_cols, tile_rows, tile_counts):
    shards = lax.axis_size(("xy", "zl"))
    quads = lax.axis_size("quad")
    local_rows, features = basis_rows.shape
    tile_size = tile_blocks.shape[-1]
    block_count = local_rows // tile_size
    blocks = basis_rows.reshape(block_count, tile_size, features)
    exchange = functools.partial(
        lax.all_to_all, split_axis=0, concat_axis=0, tiled=True
    )
    spot = jnp.stack([lax.axis_index("quad"), lax.axis_index("core")]).astype(jnp.int32)

    sent = apply_tiles(
        tile_rows[0].transpose(2, 0, 1),
        tile_counts[0, 0],
        tile_cols[0, 0],
        tile_blocks[0, 0],
        blocks,
    )
    sent, spot = lax.optimization_barrier((sent, spot))
    got = exchange(sent, ("xy", "zl"))
    keep, give = join(spot, blocks, got)
    taken = lax.ppermute(give, "core", [(0, 1), (1, 0)])
    gram = gram_rows(spot, blocks, block_count // quads)
    half = ((keep + gram) + taken).reshape(shards // 2, -1, tile_size)
    owned = exchange(half, "xy").sum(0)
    owned = exchange(owned.reshape(2 * quads, -1, tile_size), ("zl", "quad")).sum(0)
    owned = owned.reshape(-1, 2, tile_size).transpose(1, 0, 2)
    return owned.reshape(-1, features) * (1.0 / math.sqrt(local_rows * shards))


def solution(mesh):
    shards, groups = mesh.devices.shape
    fine = jax.sharding.Mesh(
        mesh.devices.reshape(shards // 2, 2, groups // 2, 2), ("xy", "zl", "quad", "core")
    )
    group = ("quad", "core")
    in_specs = (
        P(("xy","zl"), None),
        P(("xy","zl"), group, None, None, None, None),
        P(("xy","zl"), group, None),
        P(("xy","zl"), group, None, None),
        P(("xy","zl"), group, None),
    )
    out_specs = P(("xy","zl") + group, None)
    return jax.shard_map(body, mesh=fine, in_specs=in_specs, out_specs=out_specs, check_vma=False)
```
